128 devices in a mesh: row: 4 (over y), col: 16 (over x, z_lo, core), depth: 2 (over z_hi).
Axes of the slice: x: 4, y: 4, z: 4 (z_hi: 2, z_lo: 2; z = z_hi * 2 + z_lo), core: 2. Of those that a mesh axis runs over, the one named last changes fastest.
Arguments:
- features: bfloat16 [32768, 128], P(('row', 'col')), may hold values from -6 to 6
- self_weight: bfloat16 [128, 256], P(None, 'depth'), may hold values from -0.5 to 0.5
- neigh_weight: bfloat16 [128, 256], P(None, 'depth'), may hold values from -0.5 to 0.5
- bias: float32 [256], P('depth'), may hold values from -3 to 3
- cotangent: bfloat16 [32768, 256], P(('row', 'col'), 'depth'), may hold values from -6 to 6
- tile_values: bfloat16 [32768, 128, 128], P(('row', 'col', 'depth')), may hold values from -0.0625 to 0.0625
- tile_rows: int32 [128, 256], P(('row', 'col', 'depth')), may hold values from 0 to 63
- tile_cols: int32 [128, 256], P(('row', 'col', 'depth')), may hold values from 0 to 15
- tile_counts: int32 [128], P(('row', 'col', 'depth')), may hold values from 32 to 256, as said below
Outputs:
- output: bfloat16 [32768, 256], P(('row', 'col'), 'depth')
- grad_features: bfloat16 [32768, 128], P(('row', 'col', 'depth'))
- grad_self: float32 [128, 256], P(None, 'depth')
- grad_neigh: float32 [128, 256], P(None, 'depth')
- grad_bias: float32 [256], P('depth')
The draws below stay inside these ranges and needn't reach their ends.
Inputs may be any that keep to these rules, and one draw needn't show every extreme that they name: `tile_rows`: a row block below 64. `tile_cols`: a column block below 16. `tile_counts`: each device's count is 256 divided by 1, 2, 4 or 8; some device has all 256 slots live.
All inputs are finite; a program needn't handle non-finite values.
Results may differ from the reference program's by a relative error of at most 0.0057.
Values may be sent and summed in bfloat16 or wider, within the bound.
No kernel may reach another device: no remote copies, remote signals or barrier semaphores. Data moves between devices by JAX's collectives and lax.ppermute only.
A program may use at most 64 MiB of HBM per device.

```python
import jax
import jax.numpy as jnp
from jax import lax

F = 128
H = 256
BLOCK = 128
SPAN = 512
TILES_DEV = 256
NODES = 32768
N_ROW = 4
N_COL = 16
N_DEPTH = 2


def draw_tile_counts(key, part):
    device_total = N_ROW * N_COL * N_DEPTH
    first_key, second_key = jax.random.split(jax.random.fold_in(key, 31))
    shifts = jax.random.randint(first_key, (device_total,), 0, 4, dtype=jnp.int32)
    counts = jnp.right_shift(jnp.full((device_total,), TILES_DEV, jnp.int32), shifts)
    busiest = jax.random.randint(second_key, (), 0, device_total, dtype=jnp.int32)
    counts = counts.at[busiest].set(TILES_DEV)
    return counts.astype(jnp.int32)


def place_ends(values, stream_key, low, high):
    shape = values.shape
    index_at = [jax.random.randint(jax.random.fold_in(stream_key, axis), (), 0, shape[axis]) for axis in range(len(shape))]
    values = values.at[tuple(index_at)].set(low)
    longest = shape.index(max(shape))
    index_at[longest] = (index_at[longest] + 1) % shape[longest]
    return values.at[tuple(index_at)].set(high)


def level_of(own_key, extent, shards, low, high):
    level = 1.0
    for position, parts in shards:
        heights = jax.random.uniform(jax.random.fold_in(jax.random.fold_in(own_key, 6), position), (parts,), jnp.float32, low / len(shards), high / len(shards))
        level = level * jnp.repeat(jnp.exp(heights), extent[position] // parts).reshape((-1,) + (1,) * (len(extent) - 1 - position))
    return level


def centred(stream_key, shape, scale, limit, shards=(), kind=jnp.bfloat16):
    loudness = level_of(stream_key, shape, shards, -0.22, 0.18) if shards else 1.0
    values = jax.random.normal(stream_key, shape, jnp.float32) * scale * loudness
    return jnp.minimum(jnp.maximum(values, -limit), limit).astype(kind)


def setup_inputs(seed: int = 0) -> dict:
    streams_of = jax.random.split(jax.random.key(seed), 10)
    return {
        "features": centred(streams_of[0], (NODES, F), 1.0, 6.0, ((0, 64),)),
        "self_weight": centred(streams_of[1], (F, H), F ** -0.5, 0.5, ((1, 2),)),
        "neigh_weight": centred(streams_of[2], (F, H), F ** -0.5, 0.5, ((1, 2),)),
        "bias": centred(streams_of[3], (H,), 0.5, 3.0, ((0, 2),), jnp.float32),
        "cotangent": centred(streams_of[4], (NODES, H), 1.0, 6.0, ((0, 64), (1, 2))),
        "tile_values": centred(streams_of[5], (N_ROW * N_COL * N_DEPTH * TILES_DEV, BLOCK, BLOCK), (TILES_DEV * BLOCK * BLOCK // SPAN) ** -0.5, 0.0625, ((0, 128),)),
        "tile_rows": place_ends(jax.random.randint(streams_of[6], (N_ROW * N_COL * N_DEPTH, TILES_DEV), 0, SPAN * N_COL // BLOCK), jax.random.fold_in(streams_of[6], 1), 0, (SPAN * N_COL // BLOCK) - 1).astype(jnp.int32),
        "tile_cols": place_ends(jax.random.randint(streams_of[7], (N_ROW * N_COL * N_DEPTH, TILES_DEV), 0, SPAN * N_ROW // BLOCK), jax.random.fold_in(streams_of[7], 1), 0, (SPAN * N_ROW // BLOCK) - 1).astype(jnp.int32),
        "tile_counts": draw_tile_counts(jax.random.fold_in(streams_of[9], 71), 0),
    }


def reference(features, self_weight, neigh_weight, bias, cotangent, tile_values, tile_rows, tile_cols, tile_counts):
    node_total = features.shape[0]
    hidden = self_weight.shape[1]
    blocks_span = SPAN // BLOCK
    block_total = node_total // BLOCK
    device_total = N_ROW * N_COL * N_DEPTH
    device_ids = jnp.arange(device_total, dtype=jnp.int32)
    group_row = device_ids // (N_COL * N_DEPTH)
    group_col = device_ids // N_DEPTH % N_COL
    out_block = (group_row[:, None] * (N_COL * blocks_span) + tile_rows).astype(jnp.int32)
    in_block = ((tile_cols // blocks_span * N_COL + group_col[:, None]) * blocks_span + tile_cols % blocks_span).astype(jnp.int32)
    live_mask = jnp.arange(TILES_DEV, dtype=jnp.int32)[None, :] < tile_counts[:, None]
    tile_stack = tile_values.reshape(device_total, TILES_DEV, BLOCK, BLOCK)
    transformed = jnp.dot(features, neigh_weight, preferred_element_type=jnp.float32).astype(jnp.bfloat16)
    source = transformed.reshape(block_total, BLOCK, hidden)

    def forward_step(totals, item):
        tile_block, out_index, in_index, alive = item
        product = jnp.einsum('tij,tjh->tih', tile_block.astype(jnp.float32), source[in_index].astype(jnp.float32))
        product = jnp.where(alive[:, None, None], product, 0.0)
        return (totals.at[out_index].add(product), None)
    aggregated, _ = lax.scan(forward_step, jnp.zeros((block_total, BLOCK, hidden), jnp.float32), (tile_stack, out_block, in_block, live_mask))
    preact = jnp.dot(features, self_weight, preferred_element_type=jnp.float32) + aggregated.reshape(node_total, hidden) + bias
    gate_value = jax.nn.sigmoid(preact)
    output = (preact * gate_value).astype(jnp.bfloat16)
    grad_pre = (cotangent.astype(jnp.float32) * gate_value * (1.0 + preact * (1.0 - gate_value))).astype(jnp.bfloat16)
    grad_source = grad_pre.reshape(block_total, BLOCK, hidden)

    def backward_step(totals, item):
        tile_block, out_index, in_index, alive = item
        product = jnp.einsum('tij,tih->tjh', tile_block.astype(jnp.float32), grad_source[out_index].astype(jnp.float32))
        product = jnp.where(alive[:, None, None], product, 0.0)
        return (totals.at[in_index].add(product), None)
    grad_sum, _ = lax.scan(backward_step, jnp.zeros((block_total, BLOCK, hidden), jnp.float32), (tile_stack, out_block, in_block, live_mask))
    grad_transformed = grad_sum.reshape(node_total, hidden).astype(jnp.bfloat16)
    grad_features = (jnp.dot(grad_pre, self_weight.T, preferred_element_type=jnp.float32) + jnp.dot(grad_transformed, neigh_weight.T, preferred_element_type=jnp.float32)).astype(jnp.bfloat16)
    grad_scale = 1.0 / jnp.sqrt(jnp.float32(node_total))
    grad_self = jnp.dot(features.T, grad_pre, preferred_element_type=jnp.float32) * grad_scale
    grad_neigh = jnp.dot(features.T, grad_transformed, preferred_element_type=jnp.float32) * grad_scale
    grad_bias = lax.optimization_barrier(jnp.sum(grad_pre.astype(jnp.float32), axis=0)) * grad_scale
    return (output, grad_features, grad_self, grad_neigh, grad_bias)
```

```python
import jax
import jax.numpy as jnp
from jax import lax
from jax.experimental import pallas as pl
from jax.experimental.pallas import tpu as pltpu
from jax.sharding import PartitionSpec as P

GROUP = 32
UNROLL = 8
F32 = jnp.float32
BF16 = jnp.bfloat16


def dot_nn(a, b):
    return lax.dot_general(a, b, (((1,), (0,)), ((), ())), preferred_element_type=F32)


def dot_nt(a, b):
    return lax.dot_general(a, b, (((1,), (1,)), ((), ())), preferred_element_type=F32)


def dot_tn(a, b):
    return lax.dot_general(a, b, (((0,), (0,)), ((), ())), preferred_element_type=F32)


def start_tiles(live_groups, tiles, tile_buf, sems):
    def start(group, carry):
        at = pl.ds(group * GROUP, GROUP)
        pltpu.make_async_copy(tiles.at[at], tile_buf.at[at], sems.at[group]).start()
        return carry

    lax.fori_loop(0, live_groups, start, 0)


def for_tiles(live_groups, tiles, tile_buf, sems, step):
    def one_group(group, carry):
        at = pl.ds(group * GROUP, GROUP)
        pltpu.make_async_copy(tiles.at[at], tile_buf.at[at], sems.at[group]).wait()

        def some(part, inner):
            for k in range(UNROLL):
                step(group * GROUP + part * UNROLL + k)
            return inner

        return lax.fori_loop(0, GROUP // UNROLL, some, carry)

    lax.fori_loop(0, live_groups, one_group, 0)


def forward_kernel(info, rows, cols, x0, x1, x2, x3, tiles, out, x_buf, tile_buf, acc, sems, x_sems):
    live_groups = info[0] // GROUP
    own_row = info[1]
    start_tiles(live_groups, tiles, tile_buf, sems)
    shards = (x0, x1, x2, x3)
    span = x0.shape[0]
    copies = [
        pltpu.make_async_copy(shard, x_buf.at[pl.ds(k * span, span)], x_sems.at[k])
        for k, shard in enumerate(shards)
    ]
    for copy in copies:
        copy.start()
    acc[...] = jnp.zeros_like(acc)
    for copy in copies:
        copy.wait()
    span_blocks = span // 128

    def step(t):
        j = cols[t]
        at = ((own_row - j // span_blocks) & 3) * span_blocks + j % span_blocks
        block = x_buf[pl.ds(pl.multiple_of(at * 128, 128), 128), :]
        target = pl.ds(pl.multiple_of(rows[t] * 128, 128), 128)
        acc[target, :] += dot_nn(tile_buf[t], block)

    for_tiles(live_groups, tiles, tile_buf, sems, step)
    out[...] = acc[...].astype(BF16)


def backward_kernel(info, rows, cols, q, tiles, out, tile_buf, acc, sems):
    live_groups = info[0] // GROUP
    start_tiles(live_groups, tiles, tile_buf, sems)
    acc[...] = jnp.zeros_like(acc)

    def step(t):
        acc[cols[t]] += dot_nn(q[rows[t]], tile_buf[t])

    for_tiles(live_groups, tiles, tile_buf, sems, step)
    out[...] = acc[...].astype(BF16)


def middle_kernel(
    depth, parts, x, ws_a, ws_b, wn_a, wn_b, b_a, b_b, cot_a, cot_b,
    out_a, out_b, q, own_term, gw_a, gw_b,
):
    total = parts[0].astype(F32)
    for k in range(1, parts.shape[0]):
        total = total + parts[k].astype(F32)
    high = total.astype(BF16)
    low = (total - high.astype(F32)).astype(BF16)
    x_val = x[...]
    grads = []
    for ws, wn, b, cot, out in ((ws_a, wn_a, b_a, cot_a, out_a), (ws_b, wn_b, b_b, cot_b, out_b)):
        wn_val = wn[...]
        pre = dot_nn(x_val, ws[...]) + (dot_nn(high, wn_val) + dot_nn(low, wn_val)) + b[...]
        gate = jax.nn.sigmoid(pre)
        out[...] = (pre * gate).astype(BF16)
        grads.append((cot[...].astype(F32) * gate * (1.0 + pre * (1.0 - gate))).astype(BF16))
    g_a, g_b = grads
    for k in range(q.shape[0]):
        at = slice(k * 128, (k + 1) * 128)
        q[k] = (dot_nt(wn_a[...], g_a[at]) + dot_nt(wn_b[...], g_b[at])).astype(BF16)
    own_term[...] = dot_nt(g_a, ws_a[...]) + dot_nt(g_b, ws_b[...])
    for g, gw in ((g_a, gw_a), (g_b, gw_b)):
        gw[0:128] = dot_tn(x_val, g)
        gw[128:256] = dot_tn(high, g) + dot_tn(low, g)
        gw[256:264] = jnp.broadcast_to(jnp.sum(g.astype(F32), axis=0, keepdims=True), (8, 128))


def finish_kernel(parts, own_term, out):
    for k in range(parts.shape[1]):
        total = parts[0, k].astype(F32)
        for m in range(1, parts.shape[0]):
            total = total + parts[m, k].astype(F32)
        at = slice(k * 128, (k + 1) * 128)
        out[at] = (total.T + own_term[at]).astype(BF16)


def body(
    features,
    self_weight,
    neigh_weight,
    bias,
    cotangent,
    tile_values,
    tile_rows,
    tile_cols,
    tile_counts,
):
    span = features.shape[0]
    half = span // 2
    slots = tile_values.shape[0]
    row_count = lax.axis_size("row")
    col_count = lax.axis_size("col")
    depth_count = lax.axis_size("depth")
    own_row = lax.axis_index("row")
    own_depth = lax.axis_index("depth")
    swap = [(0, 1), (1, 0)]
    vmem = pl.BlockSpec(memory_space=pltpu.VMEM)
    smem = pl.BlockSpec(memory_space=pltpu.SMEM)
    hbm = pl.BlockSpec(memory_space=pl.ANY)
    scratch_tiles = pltpu.VMEM((slots, 128, 128), BF16)
    tile_sems = pltpu.SemaphoreType.DMA((slots // GROUP,))

    def from_row(k):
        return lax.ppermute(features, "row", [(i, (i + k) % row_count) for i in range(row_count)])

    shards = [features] + [from_row(k) for k in range(1, row_count)]
    other_cot = lax.ppermute(
        lax.dynamic_slice_in_dim(cotangent, (1 - own_depth) * half, half, 0), "depth", swap
    )
    other_ws = lax.ppermute(self_weight, "depth", swap)
    other_wn = lax.ppermute(neigh_weight, "depth", swap)
    own_bias = bias[None, :]
    other_bias = lax.ppermute(own_bias, "depth", swap)

    info = jnp.stack([tile_counts[0], own_row.astype(jnp.int32)])
    rows = tile_rows[0]
    cols = tile_cols[0]
    group_rows = span * col_count
    partial = pl.pallas_call(
        forward_kernel,
        in_specs=[smem] * 3 + [hbm] * 5,
        out_specs=vmem,
        out_shape=jax.ShapeDtypeStruct((group_rows, 128), BF16),
        scratch_shapes=[
            pltpu.VMEM((span * row_count, 128), BF16),
            scratch_tiles,
            pltpu.VMEM((group_rows, 128), F32),
            tile_sems,
            pltpu.SemaphoreType.DMA((row_count,)),
        ],
        name="forward",
    )(info, rows, cols, *shards, tile_values)
    plane = col_count * depth_count
    parts = lax.all_to_all(partial.reshape(plane, half, 128), ("col", "depth"), 0, 0, tiled=True)

    def mine(shape):
        return pl.BlockSpec(shape, lambda i, d: (d[0], 0))

    def whole(shape):
        return pl.BlockSpec(shape, lambda i, d: (0,) * len(shape))

    out_shapes = [
        jax.ShapeDtypeStruct((half, 128), BF16),
        jax.ShapeDtypeStruct((half, 128), BF16),
        jax.ShapeDtypeStruct((half // 128, 128, 128), BF16),
        jax.ShapeDtypeStruct((half, 128), F32),
        jax.ShapeDtypeStruct((264, 128), F32),
        jax.ShapeDtypeStruct((264, 128), F32),
    ]
    weight = whole((128, 128))
    line = whole((1, 128))
    out_own, out_other, q, own_term, gw_own, gw_other = pl.pallas_call(
        middle_kernel,
        grid_spec=pltpu.PrefetchScalarGridSpec(
            num_scalar_prefetch=1,
            grid=(1,),
            in_specs=[
                whole((plane, half, 128)),
                mine((half, 128)),
                weight, weight, weight, weight, line, line,
                mine((half, 128)),
                whole((half, 128)),
            ],
            out_specs=[whole(s.shape) for s in out_shapes],
        ),
        out_shape=out_shapes,
        name="middle",
    )(
        own_depth.astype(jnp.int32)[None], parts, features, self_weight, other_ws, neigh_weight,
        other_wn, own_bias, other_bias, cotangent, other_cot,
    )
    out_received = lax.ppermute(out_other, "depth", swap)
    gw = gw_own + lax.ppermute(gw_other, "depth", swap)
    blocks = half // 128
    q_all = lax.all_to_all(
        jnp.broadcast_to(q[None], (plane, blocks, 128, 128)), ("col", "depth"), 0, 0, tiled=True
    ).reshape(plane * blocks, 128, 128)
    col_blocks = span * row_count // 128
    grad_partial = pl.pallas_call(
        backward_kernel,
        in_specs=[smem] * 3 + [vmem, hbm],
        out_specs=vmem,
        out_shape=jax.ShapeDtypeStruct((col_blocks, 128, 128), BF16),
        scratch_shapes=[scratch_tiles, pltpu.VMEM((col_blocks, 128, 128), F32), tile_sems],
        name="backward",
    )(info, rows, cols, q_all, tile_values)
    ring = row_count * depth_count
    grad_parts = lax.all_to_all(
        grad_partial.reshape(ring, blocks, 128, 128), ("row", "depth"), 0, 0, tiled=True
    )
    grad_features = pl.pallas_call(
        finish_kernel,
        in_specs=[vmem, vmem],
        out_specs=vmem,
        out_shape=jax.ShapeDtypeStruct((half, 128), BF16),
        name="finish",
    )(grad_parts, own_term)

    packed = jnp.concatenate(
        [
            gw[:256].reshape(col_count, 256 // col_count, 128),
            jnp.broadcast_to(gw[256:][None], (col_count, 8, 128)),
        ],
        axis=1,
    )
    piece = jnp.sum(lax.all_to_all(packed, "col", 0, 0, tiled=True), axis=0)
    piece = piece + sum(
        lax.ppermute(piece, "row", [(i, (i + k) % row_count) for i in range(row_count)])
        for k in range(1, row_count)
    )
    grad_scale = 1.0 / jnp.sqrt(jnp.float32(span * row_count * col_count))
    piece = piece * grad_scale
    rows_each = 256 // col_count
    full = lax.all_to_all(
        jnp.broadcast_to(piece[:rows_each][None], (col_count, rows_each, 128)),
        "col", 0, 0, tiled=True,
    ).reshape(256, 128)
    first = jnp.where(own_depth == 0, out_own, out_received)
    second = jnp.where(own_depth == 0, out_received, out_own)
    output = jnp.concatenate([first, second], axis=0)
    return (output, grad_features, full[:128], full[128:], piece[rows_each])


def solution(mesh):
    placed = (
        P(("row", "col"), None),
        P(None, "depth"),
        P(None, "depth"),
        P("depth"),
        P(("row", "col"), "depth"),
        P(("row", "col", "depth"), None, None),
        P(("row", "col", "depth"), None),
        P(("row", "col", "depth"), None),
        P(("row", "col", "depth")),
    )
    return jax.shard_map(
        body,
        mesh=mesh,
        in_specs=placed,
        out_specs=(
            P(("row", "col"), "depth"),
            P(("row", "col", "depth"), None),
            P(None, "depth"),
            P(None, "depth"),
            P("depth"),
        ),
        check_vma=False,
    )
```

```python
import jax
import jax.numpy as jnp
from jax import lax
from jax.experimental import pallas as pl
from jax.experimental.pallas import tpu as pltpu
from jax.sharding import Mesh, PartitionSpec as P


GROUP = 32
F32 = jnp.float32
BF16 = jnp.bfloat16


def dot_nn(a, b):
    return lax.dot_general(a, b, (((1,), (0,)), ((), ())), preferred_element_type=F32)


def dot_nt(a, b):
    return lax.dot_general(a, b, (((1,), (1,)), ((), ())), preferred_element_type=F32)


def dot_tn(a, b):
    return lax.dot_general(a, b, (((0,), (0,)), ((), ())), preferred_element_type=F32)


def tile_copy(group, tiles, tile_buf, sems):
    at = pl.ds(group * GROUP, GROUP)
    return pltpu.make_async_copy(tiles.at[at], tile_buf.at[at], sems.at[group])


def start_tiles(live_groups, tiles, tile_buf, sems):
    def start(group, carry):
        tile_copy(group, tiles, tile_buf, sems).start()
        return carry

    lax.fori_loop(0, live_groups, start, 0)


def for_tiles(live_groups, tiles, tile_buf, sems, step):
    def one_group(group, carry):
        tile_copy(group, tiles, tile_buf, sems).wait()
        for k in range(GROUP):
            step(group * GROUP + k)
        return carry

    lax.fori_loop(0, live_groups, one_group, 0)


def forward_kernel(
    live, into, source, x0, x1, x2, x3, tiles, acc, other, x_buf, tile_buf, sems, x_sems
):
    live_groups = live[0] // GROUP
    start_tiles(live_groups, tiles, tile_buf, sems)
    span = x0.shape[0]
    copies = [
        pltpu.make_async_copy(shard, x_buf.at[pl.ds(k * span, span)], x_sems.at[k])
        for k, shard in enumerate((x0, x1, x2, x3))
    ]
    for copy in copies:
        copy.start()
    acc[...] = jnp.zeros_like(acc)
    for copy in copies:
        copy.wait()

    def step(t):
        block = x_buf[pl.ds(pl.multiple_of(source[t] * 128, 128), 128), :]
        target = pl.ds(pl.multiple_of(into[t] * 128, 128), 128)
        acc[target, :] += dot_nn(tile_buf[t], block)

    for_tiles(live_groups, tiles, tile_buf, sems, step)
    other[...] = acc[other.shape[0] :, :].astype(BF16)


def backward_kernel(live, into, cols, q_own, q_other, tiles, out, q_buf, tile_buf, acc, sems, q_sems):
    live_groups = live[0] // GROUP
    start_tiles(live_groups, tiles, tile_buf, sems)
    half = q_own.shape[0]
    copies = [
        pltpu.make_async_copy(part, q_buf.at[pl.ds(k * half, half)], q_sems.at[k])
        for k, part in enumerate((q_own, q_other))
    ]
    for copy in copies:
        copy.start()
    acc[...] = jnp.zeros_like(acc)
    for copy in copies:
        copy.wait()

    def step(t):
        acc[cols[t]] += dot_nn(q_buf[into[t]], tile_buf[t])

    for_tiles(live_groups, tiles, tile_buf, sems, step)
    out[...] = acc[...].astype(BF16)


def pack_kernel(cot, ws, wn, bias, packed):
    half = cot.shape[0] // 2
    other = 1 - lax.axis_index("depth")
    packed[0:half] = cot[pl.ds(other * half, half), :]
    packed[half : half + 128] = ws[...]
    packed[half + 128 : half + 256] = wn[...]
    first = bias[...].astype(BF16)
    rest = bias[...] - first.astype(F32)
    second = rest.astype(BF16)
    third = (rest - second.astype(F32)).astype(BF16)
    row = lax.broadcasted_iota(jnp.int32, (16, 128), 0)
    lines = jnp.where(row == 0, first.astype(F32), jnp.where(row == 1, second.astype(F32), third.astype(F32)))
    packed[half + 256 : half + 272] = jnp.where(row < 3, lines, 0.0).astype(BF16)


def own_part(ref):
    half = ref.shape[0] // 2
    return ref[pl.ds(lax.axis_index("depth") * half, half), :]


def middle_kernel(
    parts, x, ws_a, wn_a, b_a, cot_a, packed, out_a, out_b, q, g_a, g_b, high_out, low_out
):
    total = parts[0].astype(F32)
    for k in range(1, parts.shape[0]):
        total = total + parts[k].astype(F32)
    high = total.astype(BF16)
    low = (total - high.astype(F32)).astype(BF16)
    high_out[...] = high
    low_out[...] = low
    x_val = own_part(x)
    half = x_val.shape[0]
    ws_b = packed[half : half + 128]
    wn_b = packed[half + 128 : half + 256]
    b_b = jnp.sum(packed[half + 256 : half + 272].astype(F32), axis=0, keepdims=True)
    for ws, wn, b, cot, out, g in (
        (ws_a[...], wn_a[...], b_a[...], own_part(cot_a), out_a, g_a),
        (ws_b, wn_b, b_b, packed[0:half], out_b, g_b),
    ):
        pre = dot_nn(x_val, ws) + (dot_nn(high, wn) + dot_nn(low, wn)) + b
        gate = jax.nn.sigmoid(pre)
        out[...] = (pre * gate).astype(BF16)
        g[...] = (cot.astype(F32) * gate * (1.0 + pre * (1.0 - gate))).astype(BF16)
    for k in range(q.shape[1]):
        at = slice(k * 128, (k + 1) * 128)
        block = (dot_nt(wn_a[...], g_a[at]) + dot_nt(wn_b, g_b[at])).astype(BF16)
        for copy in range(q.shape[0]):
            q[copy, k] = block


def weights_kernel(x, ws_a, packed, g_a, g_b, high, low, own_term, keep, send):
    x_val = own_part(x)
    half = x_val.shape[0]
    ws_b = packed[half : half + 128]
    own_term[...] = dot_nt(g_a[...], ws_a[...]) + dot_nt(g_b[...], ws_b)

    def fill(first, second):
        for k, g_ref in enumerate((g_a, g_b)):
            g = g_ref[...]
            first[k, 0:128] = dot_tn(x_val, g)
            second[k, 0:128] = dot_tn(high[...], g) + dot_tn(low[...], g)
            line = jnp.broadcast_to(jnp.sum(g.astype(F32), axis=0, keepdims=True), (8, 128))
            first[k, 128:136] = line
            second[k, 128:136] = line

    @pl.when(lax.axis_index("core") == 0)
    def _():
        fill(keep, send)

    @pl.when(lax.axis_index("core") == 1)
    def _():
        fill(send, keep)


def finish_kernel(parts, own_term, out):
    for k in range(parts.shape[1]):
        total = parts[0, k].astype(F32)
        for m in range(1, parts.shape[0]):
            total = total + parts[m, k].astype(F32)
        at = slice(k * 128, (k + 1) * 128)
        out[at] = (total.T + own_term[at]).astype(BF16)


def shift(value, axis, by):
    size = lax.axis_size(axis)
    return lax.ppermute(value, axis, [(i, (i + by) % size) for i in range(size)])


def sum_over(value, axis):
    size = lax.axis_size(axis)
    return value + sum(shift(value, axis, k) for k in range(1, size))


def body(
    features,
    self_weight,
    neigh_weight,
    bias,
    cotangent,
    tile_values,
    tile_rows,
    tile_cols,
    tile_counts,
):
    span = features.shape[0]
    half = span // 2
    blocks = half // 128
    slots = tile_values.shape[0]
    row_count = lax.axis_size("row")
    own_row = lax.axis_index("row")
    own_core = lax.axis_index("core")
    own_depth = lax.axis_index("depth")
    plane = ("depth", "near", "x")
    chips = lax.axis_size("x") * lax.axis_size("near") * lax.axis_size("depth")
    vmem = pl.BlockSpec(memory_space=pltpu.VMEM)
    smem = pl.BlockSpec(memory_space=pltpu.SMEM)
    hbm = pl.BlockSpec(memory_space=pl.ANY)
    scratch_tiles = pltpu.VMEM((slots, 128, 128), BF16)
    tile_sems = pltpu.SemaphoreType.DMA((slots // GROUP,))

    def in_vmem(value):
        return pltpu.with_memory_space_constraint(value, pltpu.VMEM)

    shards = [pltpu.with_memory_space_constraint(features, pltpu.HBM)] + [
        in_vmem(shift(features, "row", k)) for k in (2, 1, 3)
    ]
    own_bias = bias[None, :]
    packed = pl.pallas_call(
        pack_kernel,
        in_specs=[vmem] * 4,
        out_specs=vmem,
        out_shape=pltpu.VMEM((half + 272, 128), BF16),
        compiler_params=pltpu.CompilerParams(vmem_limit_bytes=4 * 1024 * 1024),
        name="pack",
    )(cotangent, self_weight, neigh_weight, own_bias)
    packed = shift(packed, "depth", 1)

    tiles = pltpu.with_memory_space_constraint(tile_values, pltpu.HBM)
    rows = tile_rows[0]
    cols = tile_cols[0]
    span_blocks = span // 128
    behind = (own_row - cols // span_blocks) % row_count
    source = jnp.where(behind == 1, 2, jnp.where(behind == 2, 1, behind)) * span_blocks
    source = source + cols % span_blocks
    owner = rows // blocks
    chip = owner % 2 * 8 + owner // 4 % 2 * 4 + owner // 8
    apart = (owner // 2 % 2) ^ own_core
    into = (apart * chips + chip) * blocks + rows % blocks
    half_rows = chips * half

    def build_shape(shape, dtype):
        return jax.ShapeDtypeStruct(shape, dtype)

    acc, other = pl.pallas_call(
        forward_kernel,
        in_specs=[smem] * 3 + [hbm] * 5,
        out_specs=[vmem, vmem],
        out_shape=[pltpu.VMEM((2 * half_rows, 128), F32), pltpu.VMEM((half_rows, 128), BF16)],
        scratch_shapes=[
            pltpu.VMEM((span * row_count, 128), BF16),
            scratch_tiles,
            tile_sems,
            pltpu.SemaphoreType.DMA((row_count,)),
        ],
        compiler_params=pltpu.CompilerParams(vmem_limit_bytes=16 * 1024 * 1024),
        name="forward",
    )(tile_counts, into, source, *shards, tiles)
    summed = (acc[:half_rows] + shift(other, "core", 1).astype(F32)).astype(BF16)
    parts = lax.all_to_all(summed.reshape(chips, half, 128), plane, 0, 0, tiled=True)
    parts = in_vmem(parts)

    def small_call(kernel, inputs, out_shape):
        return pl.pallas_call(
            kernel,
            in_specs=[vmem] * len(inputs),
            out_specs=[vmem] * len(out_shape),
            out_shape=out_shape,
            compiler_params=pltpu.CompilerParams(vmem_limit_bytes=12 * 1024 * 1024),
        )(*inputs)

    node_shape = build_shape((half, 128), BF16)
    out_own, out_other, q, g_a, g_b, high, low = small_call(
        middle_kernel,
        (parts, features, self_weight, neigh_weight, own_bias, cotangent, packed),
        [node_shape, node_shape, pltpu.VMEM((chips, blocks, 128, 128), BF16)] + [node_shape] * 4,
    )
    q_own = lax.all_to_all(q, plane, 0, 0, tiled=True).reshape(chips * blocks, 128, 128)
    q_own = in_vmem(q_own)
    gw_shape = build_shape((2, 136, 128), F32)
    own_term, keep, send = small_call(
        weights_kernel,
        (features, self_weight, packed, g_a, g_b, high, low),
        [build_shape((half, 128), F32), gw_shape, gw_shape],
    )
    out_received = shift(out_other, "depth", 1)
    gw = keep + shift(send, "core", 1)
    gw = sum_over(gw, "row")
    q_own, gw = lax.optimization_barrier((q_own, gw))
    q_other = in_vmem(shift(q_own, "core", 1))
    near = lax.axis_size("near")
    moves = [
        lax.ppermute(
            gw[flip],
            ("near", "depth"),
            [(n * 2 + d, (n ^ step) * 2 + (d ^ flip)) for n in range(near) for d in range(2)],
        )
        for step, flip in ((1, 0), (0, 1), (1, 1))
    ]
    gw = gw[0] + moves[0] + moves[1] + moves[2]
    gw = sum_over(gw, "x")
    col_blocks = span * row_count // 128
    grad_partial = pl.pallas_call(
        backward_kernel,
        in_specs=[smem] * 3 + [hbm] * 3,
        out_specs=vmem,
        out_shape=pltpu.VMEM((col_blocks, 128, 128), BF16),
        scratch_shapes=[
            pltpu.VMEM((2 * chips * blocks, 128, 128), BF16),
            scratch_tiles,
            pltpu.VMEM((col_blocks, 128, 128), F32),
            tile_sems,
            pltpu.SemaphoreType.DMA((2,)),
        ],
        compiler_params=pltpu.CompilerParams(vmem_limit_bytes=16 * 1024 * 1024),
        name="backward",
    )(tile_counts, into, cols, q_own, q_other, tiles)
    ring = row_count * 2
    grad_parts = in_vmem(
        lax.all_to_all(
            grad_partial.reshape(ring, blocks, 128, 128), ("row", "depth"), 0, 0, tiled=True
        )
    )
    grad_features = pl.pallas_call(
        finish_kernel,
        in_specs=[vmem, vmem],
        out_specs=vmem,
        out_shape=node_shape,
        compiler_params=pltpu.CompilerParams(vmem_limit_bytes=8 * 1024 * 1024),
        name="finish",
    )(grad_parts, own_term)

    gw = gw * (1.0 / jnp.sqrt(jnp.float32(span * row_count * 2 * chips // 2)))
    mine_gw = gw[:128]
    other_gw = shift(mine_gw, "core", 1)
    is_first = own_core == 0
    grad_self = jnp.where(is_first, mine_gw, other_gw)
    grad_neigh = jnp.where(is_first, other_gw, mine_gw)
    first = jnp.where(own_depth == 0, out_own, out_received)
    second = jnp.where(own_depth == 0, out_received, out_own)
    output = jnp.concatenate([first, second], axis=0)
    return (output, grad_features, grad_self, grad_neigh, gw[128])


def solution(mesh):
    fine = Mesh(mesh.devices.reshape(4, 4, 2, 2, 2), ("row", "x", "near", "core", "depth"))
    nodes = ("row", "x", "near", "core")
    every = nodes + ("depth",)
    placed = (
        P(nodes, None),
        P(None, "depth"),
        P(None, "depth"),
        P("depth"),
        P(nodes, "depth"),
        P(every, None, None),
        P(every, None),
        P(every, None),
        P(every),
    )

    return jax.shard_map(
        body,
        mesh=fine,
        in_specs=placed,
        out_specs=(P(nodes, "depth"), P(every, None), P(None, "depth"), P(None, "depth"), P("depth")),
        check_vma=False,
    )
```

```python
import jax
import jax.numpy as jnp
from jax import lax
from jax.experimental import pallas as pl
from jax.experimental.pallas import tpu as pltpu
from jax.sharding import Mesh, PartitionSpec as P


GROUP = 32
AHEAD = 3
HEAD = 3
F32 = jnp.float32
BF16 = jnp.bfloat16


def dot_nn(a, b):
    return lax.dot_general(a, b, (((1,), (0,)), ((), ())), preferred_element_type=F32)


def dot_nt(a, b):
    return lax.dot_general(a, b, (((1,), (1,)), ((), ())), preferred_element_type=F32)


def dot_tn(a, b):
    return lax.dot_general(a, b, (((0,), (0,)), ((), ())), preferred_element_type=F32)


def tile_copy(group, first, tiles, tile_buf, sems):
    size = pl.ds(group * GROUP, GROUP)
    at = pl.ds((group - first) * GROUP, GROUP)
    return pltpu.make_async_copy(tiles.at[size], tile_buf.at[at], sems.at[group])


def head_copies(live_groups, tiles, head, sems, act):
    for group in range(HEAD):

        @pl.when(group < live_groups)
        def _(group=group):
            copy = tile_copy(group, 0, tiles, head, sems)
            copy.start() if act == "start" else copy.wait()


def start_tail(live_groups, tiles, tail, sems):
    def start(group, carry):
        tile_copy(group, HEAD, tiles, tail, sems).start()
        return carry

    lax.fori_loop(HEAD, jnp.minimum(live_groups, HEAD + AHEAD), start, 0)


def for_tiles(live_groups, tiles, head, tail, sems, step):
    def head_group(group, carry):
        for k in range(GROUP):
            step(head[group * GROUP + k], group * GROUP + k)
        return carry

    def tail_group(group, carry):
        tile_copy(group, HEAD, tiles, tail, sems).wait()

        @pl.when(group + AHEAD < live_groups)
        def _():
            tile_copy(group + AHEAD, HEAD, tiles, tail, sems).start()

        for k in range(GROUP):
            step(tail[(group - HEAD) * GROUP + k], group * GROUP + k)
        return carry

    lax.fori_loop(0, jnp.minimum(live_groups, HEAD), head_group, 0)
    lax.fori_loop(HEAD, live_groups, tail_group, 0)


def forward_kernel(
    live, into, source, x0, x1, x2, x3, tiles, head, zeros, acc, other, x_buf, tail, sems, x_sems
):
    live_groups = live[0] // GROUP
    span = x0.shape[0]
    copies = [
        pltpu.make_async_copy(shard, x_buf.at[pl.ds(k * span, span)], x_sems.at[k])
        for k, shard in enumerate((x0, x1, x2, x3))
    ]
    for copy in copies:
        copy.start()
    start_tail(live_groups, tiles, tail, sems)
    for copy in copies:
        copy.wait()

    def step(tile, t):
        acc[into[t]] += dot_nn(tile, x_buf[source[t]])

    for_tiles(live_groups, tiles, head, tail, sems, step)
    other[...] = acc[other.shape[0] :].astype(BF16)


def ready_kernel(live, q_own, tiles, head, q_buf, sems, q_sem):
    live_groups = live[0] // GROUP
    copy = pltpu.make_async_copy(q_own, q_buf.at[pl.ds(0, q_own.shape[0])], q_sem)
    copy.start()
    head_copies(live_groups, tiles, head, sems, "start")
    copy.wait()
    head_copies(live_groups, tiles, head, sems, "wait")


def backward_kernel(
    live, into, cols, q_other, tiles, head, q_half, out, q_buf, tail, acc, sems, q_sem
):
    live_groups = live[0] // GROUP
    half = q_other.shape[0]
    copy = pltpu.make_async_copy(q_other, q_buf.at[pl.ds(half, half)], q_sem)
    copy.start()
    start_tail(live_groups, tiles, tail, sems)
    acc[...] = jnp.zeros_like(acc)
    copy.wait()

    def step(tile, t):
        acc[cols[t]] += dot_nn(q_buf[into[t]], tile)

    for_tiles(live_groups, tiles, head, tail, sems, step)
    out[...] = acc[...].astype(BF16)


def prepare_kernel(live, bias, cot, ws, wn, tiles, packed, head, acc, sems, tile_sems):
    live_groups = live[0] // GROUP
    half = cot.shape[0] // 2
    other = 1 - lax.axis_index("depth")
    copies = [
        pltpu.make_async_copy(part, packed.at[pl.ds(at, part.shape[0])], sems.at[k])
        for k, (part, at) in enumerate(
            ((cot.at[pl.ds(other * half, half)], 0), (ws, half), (wn, half + 128))
        )
    ]
    for copy in copies:
        copy.start()
    head_copies(live_groups, tiles, head, tile_sems, "start")
    first = bias[...].astype(BF16)
    rest = bias[...] - first.astype(F32)
    second = rest.astype(BF16)
    third = (rest - second.astype(F32)).astype(BF16)
    row = lax.broadcasted_iota(jnp.int32, (16, 128), 0)
    lines = jnp.where(row == 0, first.astype(F32), jnp.where(row == 1, second.astype(F32), third.astype(F32)))
    packed[half + 256 : half + 272] = jnp.where(row < 3, lines, 0.0).astype(BF16)
    acc[...] = jnp.zeros_like(acc)
    for copy in copies:
        copy.wait()
    head_copies(live_groups, tiles, head, tile_sems, "wait")


def own_part(ref):
    half = ref.shape[0] // 2
    return ref[pl.ds(lax.axis_index("depth") * half, half), :]


def middle_kernel(
    parts, x, ws_a, wn_a, b_a, cot_a, packed, out_a, out_b, q, g_a, g_b, high_out, low_out
):
    total = parts[0].astype(F32)
    for k in range(1, parts.shape[0]):
        total = total + parts[k].astype(F32)
    high = total.astype(BF16)
    low = (total - high.astype(F32)).astype(BF16)
    high_out[...] = high
    low_out[...] = low
    x_val = own_part(x)
    half = x_val.shape[0]
    ws_b = packed[half : half + 128]
    wn_b = packed[half + 128 : half + 256]
    b_b = jnp.sum(packed[half + 256 : half + 272].astype(F32), axis=0, keepdims=True)
    for ws, wn, b, cot, out, g in (
        (ws_a[...], wn_a[...], b_a[...], own_part(cot_a), out_a, g_a),
        (ws_b, wn_b, b_b, packed[0:half], out_b, g_b),
    ):
        pre = dot_nn(x_val, ws) + (dot_nn(high, wn) + dot_nn(low, wn)) + b
        gate = jax.nn.sigmoid(pre)
        out[...] = (pre * gate).astype(BF16)
        g[...] = (cot.astype(F32) * gate * (1.0 + pre * (1.0 - gate))).astype(BF16)
    for k in range(q.shape[1]):
        at = slice(k * 128, (k + 1) * 128)
        block = (dot_nt(wn_a[...], g_a[at]) + dot_nt(wn_b, g_b[at])).astype(BF16)
        for copy in range(q.shape[0]):
            q[copy, k] = block


def weights_kernel(x, ws_a, packed, g_a, g_b, high, low, own_term, keep, send):
    x_val = own_part(x)
    half = x_val.shape[0]
    ws_b = packed[half : half + 128]
    own_term[...] = dot_nt(g_a[...], ws_a[...]) + dot_nt(g_b[...], ws_b)

    def fill(first, second):
        for k, g_ref in enumerate((g_a, g_b)):
            g = g_ref[...]
            first[k, 0:128] = dot_tn(x_val, g)
            second[k, 0:128] = dot_tn(high[...], g) + dot_tn(low[...], g)
            line = jnp.broadcast_to(jnp.sum(g.astype(F32), axis=0, keepdims=True), (8, 128))
            first[k, 128:136] = line
            second[k, 128:136] = line

    @pl.when(lax.axis_index("core") == 0)
    def _():
        fill(keep, send)

    @pl.when(lax.axis_index("core") == 1)
    def _():
        fill(send, keep)


def finish_kernel(parts, own_term, out):
    for k in range(parts.shape[1]):
        total = parts[0, k].astype(F32)
        for m in range(1, parts.shape[0]):
            total = total + parts[m, k].astype(F32)
        at = slice(k * 128, (k + 1) * 128)
        out[at] = (total.T + own_term[at]).astype(BF16)


def shift(value, axis, by):
    size = lax.axis_size(axis)
    return lax.ppermute(value, axis, [(i, (i + by) % size) for i in range(size)])


def sum_over(value, axis):
    size = lax.axis_size(axis)
    return value + sum(shift(value, axis, k) for k in range(1, size))


def body(
    features,
    self_weight,
    neigh_weight,
    bias,
    cotangent,
    tile_values,
    tile_rows,
    tile_cols,
    tile_counts,
):
    span = features.shape[0]
    half = span // 2
    blocks = half // 128
    slots = tile_values.shape[0]
    row_count = lax.axis_size("row")
    own_row = lax.axis_index("row")
    own_core = lax.axis_index("core")
    own_depth = lax.axis_index("depth")
    plane = ("near", "depth", "x")
    chips = lax.axis_size("x") * lax.axis_size("near") * lax.axis_size("depth")
    vmem = pl.BlockSpec(memory_space=pltpu.VMEM)
    smem = pl.BlockSpec(memory_space=pltpu.SMEM)
    hbm = pl.BlockSpec(memory_space=pl.ANY)
    tile_sems = pltpu.SemaphoreType.DMA((slots // GROUP,))

    def in_vmem(value):
        return pltpu.with_memory_space_constraint(value, pltpu.VMEM)

    moved = [features] + [shift(features, "row", k) for k in (2, 1, 3)]
    moved = [value.reshape(span // 128, 128, 128) for value in moved]
    shards = [pltpu.with_memory_space_constraint(moved[0], pltpu.HBM)]
    shards += [in_vmem(value) for value in moved[1:]]
    own_bias = bias[None, :]

    def in_hbm(value):
        return pltpu.with_memory_space_constraint(value, pltpu.HBM)

    tiles = in_hbm(tile_values)
    head_shape = pltpu.VMEM((HEAD * GROUP, 128, 128), BF16)
    tail_scratch = pltpu.VMEM((slots - HEAD * GROUP, 128, 128), BF16)
    packed, head, zeros = pl.pallas_call(
        prepare_kernel,
        in_specs=[smem, vmem] + [hbm] * 4,
        out_specs=[vmem] * 3,
        out_shape=[
            pltpu.VMEM((half + 272, 128), BF16),
            head_shape,
            pltpu.VMEM((2 * chips * blocks, 128, 128), F32),
        ],
        scratch_shapes=[pltpu.SemaphoreType.DMA((3,)), tile_sems],
        compiler_params=pltpu.CompilerParams(vmem_limit_bytes=2 * 1024 * 1024),
        name="prepare",
    )(
        tile_counts, in_hbm(own_bias), in_hbm(cotangent), in_hbm(self_weight),
        in_hbm(neigh_weight), tiles,
    )
    packed = shift(packed, "depth", 1)

    rows = tile_rows[0]
    cols = tile_cols[0]
    span_blocks = span // 128
    behind = (own_row - cols // span_blocks) % row_count
    source = jnp.where(behind == 1, 2, jnp.where(behind == 2, 1, behind)) * span_blocks
    source = source + cols % span_blocks
    owner = rows // blocks
    part = {"depth": owner % 2, "near": owner // 4 % 2, "x": owner // 8}
    chip = 0
    for axis in plane:
        chip = chip * lax.axis_size(axis) + part[axis]
    apart = (owner // 2 % 2) ^ own_core
    into = (apart * chips + chip) * blocks + rows % blocks

    def build_shape(shape, dtype):
        return jax.ShapeDtypeStruct(shape, dtype)

    acc, other = pl.pallas_call(
        forward_kernel,
        in_specs=[smem] * 3 + [hbm] * 5 + [vmem] * 2,
        input_output_aliases={9: 0},
        out_specs=[vmem, vmem],
        out_shape=[
            pltpu.VMEM((2 * chips * blocks, 128, 128), F32),
            pltpu.VMEM((chips * blocks, 128, 128), BF16),
        ],
        scratch_shapes=[
            pltpu.VMEM((span * row_count // 128, 128, 128), BF16),
            tail_scratch,
            tile_sems,
            pltpu.SemaphoreType.DMA((row_count,)),
        ],
        compiler_params=pltpu.CompilerParams(vmem_limit_bytes=16 * 1024 * 1024),
        name="forward",
    )(tile_counts, into, source, *shards, tiles, in_vmem(head), in_vmem(zeros))
    other = shift(other, "core", 1)
    summed = (acc[: chips * blocks] + other.astype(F32)).astype(BF16)
    parts = lax.all_to_all(summed.reshape(chips, half, 128), plane, 0, 0, tiled=True)
    parts = in_vmem(parts)

    def small_call(kernel, inputs, out_shape):
        return pl.pallas_call(
            kernel,
            in_specs=[vmem] * len(inputs),
            out_specs=[vmem] * len(out_shape),
            out_shape=out_shape,
            compiler_params=pltpu.CompilerParams(vmem_limit_bytes=12 * 1024 * 1024),
        )(*inputs)

    node_shape = build_shape((half, 128), BF16)
    out_own, out_other, q, g_a, g_b, high, low = small_call(
        middle_kernel,
        (parts, features, self_weight, neigh_weight, own_bias, cotangent, packed),
        [node_shape, node_shape, pltpu.VMEM((chips, blocks, 128, 128), BF16)] + [node_shape] * 4,
    )
    q_own = lax.all_to_all(q, plane, 0, 0, tiled=True).reshape(chips * blocks, 128, 128)
    q_own = in_vmem(q_own)
    gw_shape = build_shape((2, 136, 128), F32)
    own_term, keep, send = small_call(
        weights_kernel,
        (features, self_weight, packed, g_a, g_b, high, low),
        [build_shape((half, 128), F32), gw_shape, gw_shape],
    )
    out_received = shift(out_other, "depth", 1)
    gw = keep + shift(send, "core", 1)
    sent = gw.astype(BF16)
    gw = gw + sum(shift(sent, "row", k).astype(F32) for k in range(1, row_count))
    q_own, gw = lax.optimization_barrier((q_own, gw))
    q_other = in_vmem(shift(q_own, "core", 1))
    near = lax.axis_size("near")
    moves = [
        lax.ppermute(
            gw[flip],
            ("near", "depth"),
            [(n * 2 + d, (n ^ step) * 2 + (d ^ flip)) for n in range(near) for d in range(2)],
        )
        for step, flip in ((1, 0), (0, 1), (1, 1))
    ]
    gw = gw[0] + moves[0] + moves[1] + moves[2]
    gw = sum_over(gw, "x")
    col_blocks = span * row_count // 128
    q_shape = pltpu.VMEM((2 * chips * blocks, 128, 128), BF16)
    head, q_buf = pl.pallas_call(
        ready_kernel,
        in_specs=[smem, vmem, hbm],
        out_specs=[vmem] * 2,
        out_shape=[head_shape, q_shape],
        scratch_shapes=[tile_sems, pltpu.SemaphoreType.DMA],
        compiler_params=pltpu.CompilerParams(vmem_limit_bytes=2 * 1024 * 1024),
        name="ready",
    )(tile_counts, q_own, tiles)
    grad_partial, _ = pl.pallas_call(
        backward_kernel,
        in_specs=[smem] * 3 + [vmem, hbm, vmem, vmem],
        input_output_aliases={6: 1},
        out_specs=[vmem] * 2,
        out_shape=[pltpu.VMEM((col_blocks, 128, 128), BF16), q_shape],
        scratch_shapes=[
            tail_scratch,
            pltpu.VMEM((col_blocks, 128, 128), F32),
            tile_sems,
            pltpu.SemaphoreType.DMA,
        ],
        compiler_params=pltpu.CompilerParams(vmem_limit_bytes=16 * 1024 * 1024),
        name="backward",
    )(tile_counts, into, cols, q_other, tiles, in_vmem(head), in_vmem(q_buf))
    ring = row_count * 2
    grad_parts = in_vmem(
        lax.all_to_all(
            grad_partial.reshape(ring, blocks, 128, 128), ("row", "depth"), 0, 0, tiled=True
        )
    )
    grad_features = pl.pallas_call(
        finish_kernel,
        in_specs=[vmem, vmem],
        out_specs=vmem,
        out_shape=node_shape,
        compiler_params=pltpu.CompilerParams(vmem_limit_bytes=8 * 1024 * 1024),
        name="finish",
    )(grad_parts, own_term)

    gw = gw * (1.0 / jnp.sqrt(jnp.float32(span * row_count * 2 * chips // 2)))
    mine_gw = gw[:128]
    other_gw = shift(mine_gw, "core", 1)
    is_first = own_core == 0
    grad_self = jnp.where(is_first, mine_gw, other_gw)
    grad_neigh = jnp.where(is_first, other_gw, mine_gw)
    first = jnp.where(own_depth == 0, out_own, out_received)
    second = jnp.where(own_depth == 0, out_received, out_own)
    output = jnp.concatenate([first, second], axis=0)
    return (output, grad_features, grad_self, grad_neigh, gw[128])


def solution(mesh):
    fine = Mesh(mesh.devices.reshape(4, 4, 2, 2, 2), ("row", "x", "near", "core", "depth"))
    nodes = ("row", "x", "near", "core")
    every = nodes + ("depth",)
    placed = (
        P(nodes, None),
        P(None, "depth"),
        P(None, "depth"),
        P("depth"),
        P(nodes, "depth"),
        P(every, None, None),
        P(every, None),
        P(every, None),
        P(every),
    )

    return jax.shard_map(
        body,
        mesh=fine,
        in_specs=placed,
        out_specs=(P(nodes, "depth"), P(every, None), P(None, "depth"), P(None, "depth"), P("depth")),
        check_vma=False,
    )
```

```python
import jax
import jax.numpy as jnp
from jax import lax
from jax.experimental import pallas as pl
from jax.experimental.pallas import tpu as pltpu
from jax.sharding import Mesh, PartitionSpec as P


GROUP = 32
AHEAD = 3
HEAD = 3
F32 = jnp.float32
BF16 = jnp.bfloat16


def dot_nn(a, b):
    return lax.dot_general(a, b, (((1,), (0,)), ((), ())), preferred_element_type=F32)


def dot_nt(a, b):
    return lax.dot_general(a, b, (((1,), (1,)), ((), ())), preferred_element_type=F32)


def dot_tn(a, b):
    return lax.dot_general(a, b, (((0,), (0,)), ((), ())), preferred_element_type=F32)


def tile_copy(group, first, tiles, tile_buf, sems):
    size = pl.ds(group * GROUP, GROUP)
    at = pl.ds((group - first) * GROUP, GROUP)
    return pltpu.make_async_copy(tiles.at[size], tile_buf.at[at], sems.at[group])


def head_copies(live_groups, tiles, head, sems, act):
    for group in range(HEAD):

        @pl.when(group < live_groups)
        def _(group=group):
            copy = tile_copy(group, 0, tiles, head, sems)
            copy.start() if act == "start" else copy.wait()


def start_tail(live_groups, tiles, tail, sems):
    def start(group, carry):
        tile_copy(group, HEAD, tiles, tail, sems).start()
        return carry

    lax.fori_loop(HEAD, jnp.minimum(live_groups, HEAD + AHEAD), start, 0)


def for_tiles(live_groups, tiles, head, tail, sems, step):
    def head_group(group, carry):
        for k in range(GROUP):
            step(head[group * GROUP + k], group * GROUP + k)
        return carry

    def tail_group(group, carry):
        tile_copy(group, HEAD, tiles, tail, sems).wait()

        @pl.when(group + AHEAD < live_groups)
        def _():
            tile_copy(group + AHEAD, HEAD, tiles, tail, sems).start()

        for k in range(GROUP):
            step(tail[(group - HEAD) * GROUP + k], group * GROUP + k)
        return carry

    lax.fori_loop(0, jnp.minimum(live_groups, HEAD), head_group, 0)
    lax.fori_loop(HEAD, live_groups, tail_group, 0)


def forward_kernel(
    live, into, source, x0, x1, x2, x3, tiles, head, zeros, acc, other, x_buf, tail, sems, x_sems
):
    live_groups = live[0] // GROUP
    span = x0.shape[0]
    copies = [
        pltpu.make_async_copy(shard, x_buf.at[pl.ds(k * span, span)], x_sems.at[k])
        for k, shard in enumerate((x0, x1, x2, x3))
    ]
    for copy in copies:
        copy.start()
    start_tail(live_groups, tiles, tail, sems)
    for copy in copies:
        copy.wait()

    def step(tile, t):
        acc[into[t]] += dot_nn(tile, x_buf[source[t]])

    for_tiles(live_groups, tiles, head, tail, sems, step)
    other[...] = acc[other.shape[0] :].astype(BF16)


def ready_kernel(live, q_own, tiles, head, q_buf, sems, q_sem):
    live_groups = live[0] // GROUP
    copy = pltpu.make_async_copy(q_own, q_buf.at[pl.ds(0, q_own.shape[0])], q_sem)
    copy.start()
    head_copies(live_groups, tiles, head, sems, "start")
    copy.wait()
    head_copies(live_groups, tiles, head, sems, "wait")


def backward_kernel(
    live, into, cols, q_other, tiles, head, q_half, out, q_buf, tail, acc, sems, q_sem
):
    live_groups = live[0] // GROUP
    half = q_other.shape[0]
    copy = pltpu.make_async_copy(q_other, q_buf.at[pl.ds(half, half)], q_sem)
    copy.start()
    start_tail(live_groups, tiles, tail, sems)
    acc[...] = jnp.zeros_like(acc)
    copy.wait()

    def step(tile, t):
        acc[cols[t]] += dot_nn(q_buf[into[t]], tile)

    for_tiles(live_groups, tiles, head, tail, sems, step)
    out[...] = acc[...].astype(BF16)


def prepare_kernel(live, bias, cot, ws, wn, tiles, packed, head, acc, sems, tile_sems):
    live_groups = live[0] // GROUP
    half = cot.shape[0] // 2
    other = 1 - lax.axis_index("depth")
    copies = [
        pltpu.make_async_copy(part, packed.at[pl.ds(at, part.shape[0])], sems.at[k])
        for k, (part, at) in enumerate(
            ((cot.at[pl.ds(other * half, half)], 0), (ws, half), (wn, half + 128))
        )
    ]
    for copy in copies:
        copy.start()
    head_copies(live_groups, tiles, head, tile_sems, "start")
    first = bias[...].astype(BF16)
    rest = bias[...] - first.astype(F32)
    second = rest.astype(BF16)
    third = (rest - second.astype(F32)).astype(BF16)
    row = lax.broadcasted_iota(jnp.int32, (16, 128), 0)
    lines = jnp.where(row == 0, first.astype(F32), jnp.where(row == 1, second.astype(F32), third.astype(F32)))
    packed[half + 256 : half + 272] = jnp.where(row < 3, lines, 0.0).astype(BF16)
    acc[...] = jnp.zeros_like(acc)
    for copy in copies:
        copy.wait()
    head_copies(live_groups, tiles, head, tile_sems, "wait")


def own_part(ref):
    half = ref.shape[0] // 2
    return ref[pl.ds(lax.axis_index("depth") * half, half), :]


def middle_kernel(
    parts, x, ws_a, wn_a, b_a, cot_a, packed, out_a, out_b, q, g_a, g_b, high_out, low_out
):
    total = parts[0].astype(F32)
    for k in range(1, parts.shape[0]):
        total = total + parts[k].astype(F32)
    high = total.astype(BF16)
    low = (total - high.astype(F32)).astype(BF16)
    high_out[...] = high
    low_out[...] = low
    x_val = own_part(x)
    half = x_val.shape[0]
    ws_b = packed[half : half + 128]
    wn_b = packed[half + 128 : half + 256]
    b_b = jnp.sum(packed[half + 256 : half + 272].astype(F32), axis=0, keepdims=True)
    for ws, wn, b, cot, out, g in (
        (ws_a[...], wn_a[...], b_a[...], own_part(cot_a), out_a, g_a),
        (ws_b, wn_b, b_b, packed[0:half], out_b, g_b),
    ):
        pre = dot_nn(x_val, ws) + (dot_nn(high, wn) + dot_nn(low, wn)) + b
        gate = jax.nn.sigmoid(pre)
        out[...] = (pre * gate).astype(BF16)
        g[...] = (cot.astype(F32) * gate * (1.0 + pre * (1.0 - gate))).astype(BF16)
    for k in range(q.shape[1]):
        at = slice(k * 128, (k + 1) * 128)
        block = (dot_nt(wn_a[...], g_a[at]) + dot_nt(wn_b, g_b[at])).astype(BF16)
        for copy in range(q.shape[0]):
            q[copy, k] = block


def weights_kernel(x, ws_a, packed, g_a, g_b, high, low, own_term, keep, send):
    x_val = own_part(x)
    half = x_val.shape[0]
    ws_b = packed[half : half + 128]
    own_term[...] = dot_nt(g_a[...], ws_a[...]) + dot_nt(g_b[...], ws_b)

    def fill(first, second):
        for k, g_ref in enumerate((g_a, g_b)):
            g = g_ref[...]
            first[k, 0:128] = dot_tn(x_val, g)
            second[k, 0:128] = dot_tn(high[...], g) + dot_tn(low[...], g)
            line = jnp.broadcast_to(jnp.sum(g.astype(F32), axis=0, keepdims=True), (8, 128))
            first[k, 128:136] = line
            second[k, 128:136] = line

    @pl.when(lax.axis_index("core") == 0)
    def _():
        fill(keep, send)

    @pl.when(lax.axis_index("core") == 1)
    def _():
        fill(send, keep)


def finish_kernel(parts, own_term, out):
    for k in range(parts.shape[1]):
        total = parts[0, k].astype(F32)
        for m in range(1, parts.shape[0]):
            total = total + parts[m, k].astype(F32)
        at = slice(k * 128, (k + 1) * 128)
        out[at] = (total.T + own_term[at]).astype(BF16)


def shift(value, axis, by):
    size = lax.axis_size(axis)
    return lax.ppermute(value, axis, [(i, (i + by) % size) for i in range(size)])


def sum_over(value, axis):
    size = lax.axis_size(axis)
    return value + sum(shift(value, axis, k) for k in range(1, size))


def body(
    features,
    self_weight,
    neigh_weight,
    bias,
    cotangent,
    tile_values,
    tile_rows,
    tile_cols,
    tile_counts,
):
    span = features.shape[0]
    half = span // 2
    blocks = half // 128
    slots = tile_values.shape[0]
    row_count = lax.axis_size("row")
    own_row = lax.axis_index("row")
    own_core = lax.axis_index("core")
    own_depth = lax.axis_index("depth")
    plane = ("near", "depth", "x")
    chips = lax.axis_size("x") * lax.axis_size("near") * lax.axis_size("depth")
    vmem = pl.BlockSpec(memory_space=pltpu.VMEM)
    smem = pl.BlockSpec(memory_space=pltpu.SMEM)
    hbm = pl.BlockSpec(memory_space=pl.ANY)
    tile_sems = pltpu.SemaphoreType.DMA((slots // GROUP,))

    def in_vmem(value):
        return pltpu.with_memory_space_constraint(value, pltpu.VMEM)

    moved = [features] + [shift(features, "row", k) for k in (2, 1, 3)]
    moved = [value.reshape(span // 128, 128, 128) for value in moved]
    shards = [pltpu.with_memory_space_constraint(moved[0], pltpu.HBM)]
    shards += [in_vmem(value) for value in moved[1:]]
    own_bias = bias[None, :]

    def in_hbm(value):
        return pltpu.with_memory_space_constraint(value, pltpu.HBM)

    tiles = in_hbm(tile_values)
    head_shape = pltpu.VMEM((HEAD * GROUP, 128, 128), BF16)
    tail_scratch = pltpu.VMEM((slots - HEAD * GROUP, 128, 128), BF16)
    packed, head, zeros = pl.pallas_call(
        prepare_kernel,
        in_specs=[smem, vmem] + [hbm] * 4,
        out_specs=[vmem] * 3,
        out_shape=[
            pltpu.VMEM((half + 272, 128), BF16),
            head_shape,
            pltpu.VMEM((2 * chips * blocks, 128, 128), F32),
        ],
        scratch_shapes=[pltpu.SemaphoreType.DMA((3,)), tile_sems],
        compiler_params=pltpu.CompilerParams(vmem_limit_bytes=2 * 1024 * 1024),
        name="prepare",
    )(
        tile_counts, in_hbm(own_bias), in_hbm(cotangent), in_hbm(self_weight),
        in_hbm(neigh_weight), tiles,
    )
    packed = shift(packed, "depth", 1)

    rows = tile_rows[0]
    cols = tile_cols[0]
    span_blocks = span // 128
    behind = (own_row - cols // span_blocks) % row_count
    source = jnp.where(behind == 1, 2, jnp.where(behind == 2, 1, behind)) * span_blocks
    source = source + cols % span_blocks
    owner = rows // blocks
    part = {"depth": owner % 2, "near": owner // 4 % 2, "x": owner // 8}
    chip = 0
    for axis in plane:
        chip = chip * lax.axis_size(axis) + part[axis]
    apart = (owner // 2 % 2) ^ own_core
    into = (apart * chips + chip) * blocks + rows % blocks

    def build_shape(shape, dtype):
        return jax.ShapeDtypeStruct(shape, dtype)

    acc, other = pl.pallas_call(
        forward_kernel,
        in_specs=[smem] * 3 + [hbm] * 5 + [vmem] * 2,
        input_output_aliases={9: 0},
        out_specs=[vmem, vmem],
        out_shape=[
            pltpu.VMEM((2 * chips * blocks, 128, 128), F32),
            pltpu.VMEM((chips * blocks, 128, 128), BF16),
        ],
        scratch_shapes=[
            pltpu.VMEM((span * row_count // 128, 128, 128), BF16),
            tail_scratch,
            tile_sems,
            pltpu.SemaphoreType.DMA((row_count,)),
        ],
        compiler_params=pltpu.CompilerParams(vmem_limit_bytes=16 * 1024 * 1024),
        name="forward",
    )(tile_counts, into, source, *shards, tiles, in_vmem(head), in_vmem(zeros))
    other = shift(other, "core", 1)
    summed = (acc[: chips * blocks] + other.astype(F32)).astype(BF16)
    parts = lax.all_to_all(summed.reshape(chips, half, 128), plane, 0, 0, tiled=True)
    parts = in_vmem(parts)

    def small_call(kernel, inputs, out_shape):
        return pl.pallas_call(
            kernel,
            in_specs=[vmem] * len(inputs),
            out_specs=[vmem] * len(out_shape),
            out_shape=out_shape,
            compiler_params=pltpu.CompilerParams(vmem_limit_bytes=12 * 1024 * 1024),
        )(*inputs)

    node_shape = build_shape((half, 128), BF16)
    out_own, out_other, q, g_a, g_b, high, low = small_call(
        middle_kernel,
        (parts, features, self_weight, neigh_weight, own_bias, cotangent, packed),
        [node_shape, node_shape, pltpu.VMEM((chips, blocks, 128, 128), BF16)] + [node_shape] * 4,
    )
    q_own = lax.all_to_all(q, plane, 0, 0, tiled=True).reshape(chips * blocks, 128, 128)
    q_own = in_vmem(q_own)
    gw_shape = build_shape((2, 136, 128), F32)
    own_term, keep, send = small_call(
        weights_kernel,
        (features, self_weight, packed, g_a, g_b, high, low),
        [build_shape((half, 128), F32), gw_shape, gw_shape],
    )
    out_received = shift(out_other, "depth", 1)
    gw = keep + shift(send, "core", 1)
    sent = gw.astype(BF16)
    gw = gw + sum(shift(sent, "row", k).astype(F32) for k in range(1, row_count))
    gw = gw + shift(gw.astype(BF16), "near", 1).astype(F32)
    q_own, gw = lax.optimization_barrier((q_own, gw))
    q_other = in_vmem(shift(q_own, "core", 1))
    moved_gw = shift(gw[1], "depth", 1)
    gw = gw[0] + moved_gw
    gw = sum_over(gw, "x")
    col_blocks = span * row_count // 128
    q_shape = pltpu.VMEM((2 * chips * blocks, 128, 128), BF16)
    head, q_buf = pl.pallas_call(
        ready_kernel,
        in_specs=[smem, vmem, hbm],
        out_specs=[vmem] * 2,
        out_shape=[head_shape, q_shape],
        scratch_shapes=[tile_sems, pltpu.SemaphoreType.DMA],
        compiler_params=pltpu.CompilerParams(vmem_limit_bytes=2 * 1024 * 1024),
        name="ready",
    )(tile_counts, q_own, tiles)
    grad_partial, _ = pl.pallas_call(
        backward_kernel,
        in_specs=[smem] * 3 + [vmem, hbm, vmem, vmem],
        input_output_aliases={6: 1},
        out_specs=[vmem] * 2,
        out_shape=[pltpu.VMEM((col_blocks, 128, 128), BF16), q_shape],
        scratch_shapes=[
            tail_scratch,
            pltpu.VMEM((col_blocks, 128, 128), F32),
            tile_sems,
            pltpu.SemaphoreType.DMA,
        ],
        compiler_params=pltpu.CompilerParams(vmem_limit_bytes=16 * 1024 * 1024),
        name="backward",
    )(tile_counts, into, cols, q_other, tiles, in_vmem(head), in_vmem(q_buf))
    ring = row_count * 2
    grad_parts = in_vmem(
        lax.all_to_all(
            grad_partial.reshape(ring, blocks, 128, 128), ("row", "depth"), 0, 0, tiled=True
        )
    )
    grad_features = pl.pallas_call(
        finish_kernel,
        in_specs=[vmem, vmem],
        out_specs=vmem,
        out_shape=node_shape,
        compiler_params=pltpu.CompilerParams(vmem_limit_bytes=8 * 1024 * 1024),
        name="finish",
    )(grad_parts, own_term)

    gw = gw * (1.0 / jnp.sqrt(jnp.float32(span * row_count * 2 * chips // 2)))
    mine_gw = gw[:128]
    other_gw = shift(mine_gw, "core", 1)
    is_first = own_core == 0
    grad_self = jnp.where(is_first, mine_gw, other_gw)
    grad_neigh = jnp.where(is_first, other_gw, mine_gw)
    first = jnp.where(own_depth == 0, out_own, out_received)
    second = jnp.where(own_depth == 0, out_received, out_own)
    output = jnp.concatenate([first, second], axis=0)
    return (output, grad_features, grad_self, grad_neigh, gw[128])


def solution(mesh):
    fine = Mesh(mesh.devices.reshape(4, 4, 2, 2, 2), ("row", "x", "near", "core", "depth"))
    nodes = ("row", "x", "near", "core")
    every = nodes + ("depth",)
    placed = (
        P(nodes, None),
        P(None, "depth"),
        P(None, "depth"),
        P("depth"),
        P(nodes, "depth"),
        P(every, None, None),
        P(every, None),
        P(every, None),
        P(every),
    )

    return jax.shard_map(
        body,
        mesh=fine,
        in_specs=placed,
        out_specs=(P(nodes, "depth"), P(every, None), P(None, "depth"), P(None, "depth"), P("depth")),
        check_vma=False,
    )
```
